32 devices in a mesh: alpha: 4 (over y, x), beta: 8 (over z, core).
Axes of the slice: x: 2, y: 2, z: 4, core: 2. Of those that a mesh axis runs over, the one named last changes fastest.
Arguments:
- ci_vector: float32 [3584, 7168], P('alpha', 'beta'), may hold values from -6 to 6
- diagonal: float32 [3584, 7168], P('alpha', 'beta'), may hold values from -1.5 to 1.5
- energy: float32 [1], replicated, may hold values from -0.5 to 0.5
- alpha_partner: int32 [4, 2], P('alpha'), may hold values from 0 to 3, as said below
- alpha_coupling: bfloat16 [4, 2, 896, 896], P('alpha'), may hold values from -0.1875 to 0.1875
- alpha_mask: int32 [4, 2, 7, 7], P('alpha'), may hold values 0 or 1
- beta_partner: int32 [8, 2], P('beta'), may hold values from 0 to 7, as said below
- beta_coupling: bfloat16 [8, 2, 896, 896], P('beta', None, 'alpha'), may hold values from -0.1875 to 0.1875
- beta_mask: int32 [8, 2, 7, 7], P('beta'), may hold values 0 or 1
Outputs:
- correction: float32 [3584, 7168], P('alpha', 'beta')
The draws below stay inside these ranges and needn't reach their ends.
Inputs may be any that keep to these rules, and one draw needn't show every extreme that they name: alpha_partner[i, s] equals i with exactly one bit of its binary index flipped, and the two partners of a tile flip different bits. beta_partner[j, s] equals j with exactly one bit of its binary index flipped, and the two partners of a tile flip different bits.
All inputs are finite; a program needn't handle non-finite values. No bound on the sum of `alpha_mask` or of `beta_mask` on one device may be relied on, other than what follows from the above.
Results may differ from the reference program's by a relative error of at most 0.0003.
Values may be sent and summed in bfloat16 or wider, within the bound.
No kernel may reach another device: no remote copies, remote signals or barrier semaphores. Data moves between devices by JAX's collectives and lax.ppermute only.
A program may use at most 128 MiB of HBM per device.

```python
import jax
import jax.numpy as jnp
from jax import lax

TILE = 896
BLOCK = 128
NBLK = 7
AT = 4
BT = 8
NA = 3584
NB = 7168


def partner_table(key, tile_count):
    bit_count = tile_count.bit_length() - 1
    top_bit = bit_count - 1
    key_group, key_offset, key_flip = jax.random.split(key, 3)
    indices = jnp.arange(tile_count, dtype=jnp.int32)
    group_bits = jax.random.randint(key_group, (2,), 0, top_bit, dtype=jnp.int32)
    upper = jnp.right_shift(indices, top_bit)
    bit_first = jnp.where(upper == 1, group_bits[1], group_bits[0])
    offsets = jax.random.randint(key_offset, (tile_count,), 1, bit_count, dtype=jnp.int32)
    bit_second = (bit_first + offsets) % bit_count
    first_partner = jnp.bitwise_xor(indices, jnp.left_shift(jnp.int32(1), bit_first))
    second_partner = jnp.bitwise_xor(indices, jnp.left_shift(jnp.int32(1), bit_second))
    flips = jax.random.randint(key_flip, (tile_count,), 0, 2, dtype=jnp.int32)
    slot_zero = jnp.where(flips == 1, second_partner, first_partner)
    slot_one = jnp.where(flips == 1, first_partner, second_partner)
    return jnp.stack([slot_zero, slot_one], axis=1).astype(jnp.int32)


def draw_alpha_partner(key, part):
    return partner_table(jax.random.fold_in(key, 11), AT)


def draw_beta_partner(key, part):
    return partner_table(jax.random.fold_in(key, 23), BT)


def plant(entries, stream_key, smallest, high):
    extent = entries.shape
    index_at = [jax.random.randint(jax.random.fold_in(stream_key, axis), (), 0, extent[axis]) for axis in range(len(extent))]
    entries = entries.at[tuple(index_at)].set(smallest)
    longest = extent.index(max(extent))
    index_at[longest] = (index_at[longest] + 1) % extent[longest]
    return entries.at[tuple(index_at)].set(high)


def block_levels(rng, dims, shards, least, largest):
    level = 1.0
    for axis_at, parts in shards:
        heights = jax.random.uniform(jax.random.fold_in(jax.random.fold_in(rng, 6), axis_at), (parts,), jnp.float32, least / len(shards), largest / len(shards))
        level = level * jnp.repeat(jnp.exp(heights), dims[axis_at] // parts).reshape((-1,) + (1,) * (len(dims) - 1 - axis_at))
    return level


def scatter_about(rng, dims, scale, bound, shards=(), held_as=jnp.bfloat16):
    loudness = block_levels(rng, dims, shards, -0.22, 0.18) if shards else 1.0
    array = jax.random.normal(rng, dims, jnp.float32) * scale * loudness
    return jnp.minimum(jnp.maximum(array, -bound), bound).astype(held_as)


def setup_inputs(seed: int = 0) -> dict:
    key_of = jax.random.split(jax.random.key(seed), 10)
    ci_vector = scatter_about(key_of[0], (NA, NB), 1.0, 6.0, ((0, 4), (1, 8)), jnp.float32)
    diagonal = jnp.clip(jax.random.uniform(key_of[1], (NA, NB), jnp.float32, -1.5, 1.5) * block_levels(key_of[1], (NA, NB), ((0, 4), (1, 8)), -0.4, 0.0), -1.5, 1.5)
    energy = jnp.clip(jax.random.uniform(key_of[2], (1,), jnp.float32, -0.5, 0.5), -0.5, 0.5)
    alpha_partner = draw_alpha_partner(jax.random.fold_in(key_of[9], 71), 0)
    alpha_coupling = scatter_about(key_of[4], (AT, 2, TILE, TILE), TILE ** -0.5, 0.1875, ((0, 4),))
    alpha_mask = plant((jax.random.randint(key_of[5], (AT, 2, NBLK, NBLK), 0, 4) < 3).astype(jnp.int32), jax.random.fold_in(key_of[5], 1), 0, 1)
    beta_partner = draw_beta_partner(jax.random.fold_in(key_of[9], 71), 0)
    beta_coupling = scatter_about(key_of[7], (BT, 2, TILE, TILE), TILE ** -0.5, 0.1875, ((0, 8), (2, 4)))
    beta_mask = plant((jax.random.randint(key_of[8], (BT, 2, NBLK, NBLK), 0, 4) < 3).astype(jnp.int32), jax.random.fold_in(key_of[8], 1), 0, 1)
    return dict(ci_vector=ci_vector, diagonal=diagonal, energy=energy, alpha_partner=alpha_partner, alpha_coupling=alpha_coupling, alpha_mask=alpha_mask, beta_partner=beta_partner, beta_coupling=beta_coupling, beta_mask=beta_mask)


def expand_mask(block_mask):
    values = block_mask.astype(jnp.float32)
    values = jnp.repeat(values, BLOCK, axis=-2)
    return jnp.repeat(values, BLOCK, axis=-1)


def reference(ci_vector, diagonal, energy, alpha_partner, alpha_coupling, alpha_mask, beta_partner, beta_coupling, beta_mask):
    highest = lax.Precision.HIGHEST

    def beta_column(column):
        summed = jnp.zeros((NA, TILE), jnp.float32)
        for slot_index in range(2):
            offset = (beta_partner[column, slot_index] * TILE).astype(jnp.int32)
            partner_cols = lax.dynamic_slice_in_dim(ci_vector, offset, TILE, 1)
            weights = beta_coupling[column, slot_index].astype(jnp.float32) * expand_mask(beta_mask[column, slot_index])
            summed = summed + jnp.dot(partner_cols, weights, precision=highest)
        return summed

    def alpha_row(row_tile):
        summed = jnp.zeros((TILE, NB), jnp.float32)
        for slot_index in range(2):
            offset = (alpha_partner[row_tile, slot_index] * TILE).astype(jnp.int32)
            partner_rows = lax.dynamic_slice_in_dim(ci_vector, offset, TILE, 0)
            weights = alpha_coupling[row_tile, slot_index].astype(jnp.float32) * expand_mask(alpha_mask[row_tile, slot_index])
            summed = summed + jnp.dot(weights.T, partner_rows, precision=highest)
        return summed

    beta_term = lax.map(beta_column, jnp.arange(BT, dtype=jnp.int32))
    beta_term = jnp.transpose(beta_term, (1, 0, 2)).reshape(NA, NB)
    alpha_term = lax.map(alpha_row, jnp.arange(AT, dtype=jnp.int32)).reshape(NA, NB)
    sigma = alpha_term + beta_term
    gap = diagonal - energy[0]
    return (sigma - energy[0] * ci_vector) * gap / (gap * gap + 0.0625)
```

```python
import jax
import jax.numpy as jnp
from jax import lax
from jax.sharding import PartitionSpec as P

BLOCK = 128
SCALE = 8192.0


def flip(value, axis, bit):
    return lax.ppermute(value, axis, [(i, i ^ bit) for i in range(lax.axis_size(axis))])


def expand_mask(block_mask):
    values = block_mask.astype(jnp.bfloat16)
    values = jnp.repeat(values, BLOCK, axis=-2)
    return jnp.repeat(values, BLOCK, axis=-1)


def pick(partner, source, weights):
    zero = jnp.zeros((), weights.dtype)
    return jnp.where(partner[0] == source, weights[0], jnp.where(partner[1] == source, weights[1], zero))


def split(value):
    value = value.astype(jnp.float32)
    high = lax.reduce_precision(value, 8, 7)
    return high.astype(jnp.bfloat16), (value - high).astype(jnp.bfloat16)


def product(left, right, dims):
    return lax.dot_general(left, right, (dims, ((), ())), preferred_element_type=jnp.float32)


def gather_rows(shard):
    size = lax.axis_size("alpha")
    index = lax.axis_index("alpha")
    held = {0: shard}
    bit = 1
    while bit < size:
        for have in list(held):
            held[have ^ bit] = flip(held[have], "alpha", bit)
        bit *= 2
    rows = shard.shape[1]
    full = jnp.zeros((shard.shape[0], rows * size, shard.shape[2]), shard.dtype)
    for away, block in held.items():
        full = lax.dynamic_update_slice(full, block, (0, (index ^ away) * rows, 0))
    return full


def cycle(value, axis, low, high, turned):
    size = lax.axis_size(axis)
    def step(i, odd):
        return i ^ (high if odd else low)
    pairs = []
    for i in range(size):
        odd = (bool(i & low) ^ bool(i & high)) ^ turned
        pairs.append((i, step(i, odd)))
    arrived = lax.ppermute(value, axis, pairs)
    index = lax.axis_index(axis)
    table = [0] * size
    for a, b in pairs:
        table[b] = a
    return arrived, jnp.array(table, jnp.int32)[index]


def local(
    ci_vector,
    diagonal,
    energy,
    alpha_partner,
    alpha_coupling,
    alpha_mask,
    beta_partner,
    beta_coupling,
    beta_mask,
):
    alpha_size = lax.axis_size("alpha")
    beta_size = lax.axis_size("beta")
    beta_bits = beta_size.bit_length() - 1
    alpha_bits = alpha_size.bit_length() - 1
    alpha_index = lax.axis_index("alpha")
    beta_index = lax.axis_index("beta")

    short = (ci_vector * SCALE).astype(jnp.float16)
    from_beta = []
    low, high = 1 << (beta_bits - 2), 1 << (beta_bits - 1)
    from_beta.append(cycle(short, "beta", low, high, False))
    from_beta.append(cycle(short, "beta", low, high, True))
    for level in range(beta_bits - 2):
        from_beta.append((flip(short, "beta", 1 << level), beta_index ^ (1 << level)))
    from_alpha = [(flip(short, "alpha", 1 << level), alpha_index ^ (1 << level)) for level in range(alpha_bits)]

    beta_weights = gather_rows(beta_coupling[0]) * expand_mask(beta_mask[0])
    alpha_weights = alpha_coupling[0] * expand_mask(alpha_mask[0])

    sigma = None
    for arrived, source in from_alpha:
        weights = pick(alpha_partner[0], source, alpha_weights)
        for part in split(arrived):
            term = product(weights, part, ((0,), (0,)))
            sigma = term if sigma is None else sigma + term
    for arrived, source in reversed(from_beta):
        weights = pick(beta_partner[0], source, beta_weights)
        for part in split(arrived):
            sigma = sigma + product(part, weights, ((1,), (0,)))
    sigma = sigma * (1.0 / SCALE)
    gap = diagonal - energy[0]
    return (sigma - energy[0] * ci_vector) * gap / (gap * gap + 0.0625)


def solution(mesh):
    return jax.shard_map(
        local,
        mesh=mesh,
        in_specs=(
            P("alpha", "beta"),
            P("alpha", "beta"),
            P(),
            P("alpha", None),
            P("alpha", None, None, None),
            P("alpha", None, None, None),
            P("beta", None),
            P("beta", None, "alpha", None),
            P("beta", None, None, None),
        ),
        out_specs=P("alpha", "beta"),
        check_vma=False,
    )
```

```python
import functools

import jax
import jax.numpy as jnp
from jax import lax
from jax.experimental import pallas as pl
from jax.experimental.pallas import tpu as pltpu
from jax.sharding import PartitionSpec as P


BLOCK = 128
SCALE = 8192.0
VMEM = pl.BlockSpec(memory_space=pltpu.VMEM)
SMEM = pl.BlockSpec(memory_space=pltpu.SMEM)
ANY = pl.BlockSpec(memory_space=pl.ANY)


def params(mib):
    return pltpu.CompilerParams(vmem_limit_bytes=mib * 2**20)


def cost(flops, moved):
    return pl.CostEstimate(flops=flops, bytes_accessed=moved, transcendentals=0)


def flip(value, axis, bit):
    return lax.ppermute(value, axis, [(i, i ^ bit) for i in range(lax.axis_size(axis))])


def short(value):
    return (value * SCALE).astype(jnp.float16)


def split(value):
    value = value.astype(jnp.float32)
    high = lax.reduce_precision(value, 8, 7)
    return high.astype(jnp.bfloat16), (value - high).astype(jnp.bfloat16)


def halves(value):
    high = value.astype(jnp.bfloat16)
    return high, (value - high.astype(jnp.float32)).astype(jnp.bfloat16)


def dot(left, right):
    return jnp.dot(left, right, preferred_element_type=jnp.float32)


def cycle_pairs(size, turned):
    low, high = size >> 2, size >> 1
    return [
        (i, i ^ (high if (bool(i & low) ^ bool(i & high)) ^ turned else low))
        for i in range(size)
    ]


def level_sources(axis, levels):
    index = lax.axis_index(axis)
    return [index ^ (1 << level) for level in levels]


def cycle_source(axis, turned):
    size = lax.axis_size(axis)
    index = lax.axis_index(axis)
    low, high = size >> 2, size >> 1
    odd = ((index // low) + (index // high)) % 2 == 1
    return index ^ (jnp.where(odd, high, low) if turned else jnp.where(odd, low, high))


def slot_of(partner_ref, source):
    return jnp.where(partner_ref[0, 0] == source, 0, jnp.where(partner_ref[0, 1] == source, 1, -1))


def masked(block, bit):
    return (block.astype(jnp.float32) * bit.astype(jnp.float32)).astype(jnp.bfloat16)


def turn_kernel(cut, mask_ref, coupling_ref, *out_refs):
    slot = pl.program_id(0)
    blocks = coupling_ref.shape[1] // BLOCK
    for u in range(blocks):
        for v in range(blocks):
            rows, cols = pl.ds(u * BLOCK, BLOCK), pl.ds(v * BLOCK, BLOCK)
            out_ref, to = (out_refs[0], u) if u < cut else (out_refs[1], u - cut)
            out_ref[0, cols, pl.ds(to * BLOCK, BLOCK)] = masked(coupling_ref[0, rows, cols], mask_ref[slot, u, v]).T


def turned_weights(mask, coupling, cut):
    slots, tile, _ = coupling.shape
    depths = (cut, tile - cut)
    return pl.pallas_call(
        functools.partial(turn_kernel, cut // BLOCK),
        grid=(slots,),
        in_specs=[SMEM, pl.BlockSpec((1, tile, tile), lambda s: (s, 0, 0))],
        out_specs=[pl.BlockSpec((1, tile, depth), lambda s: (s, 0, 0)) for depth in depths],
        out_shape=[jax.ShapeDtypeStruct((slots, tile, depth), coupling.dtype) for depth in depths],
        compiler_params=params(16),
        cost_estimate=cost(0, 4 * coupling.size),
        name="turn",
    )(mask, coupling)


def place_kernel(where, mask_ref, *refs):
    shards, out_ref, sem = refs[: len(where)], refs[len(where)], refs[len(where) + 1]
    slots, tile, _ = out_ref.shape
    copies = []
    for at, ((away, slot), shard) in enumerate(zip(where, shards)):
        depth = shard.shape[-2]
        row = pl.multiple_of((lax.axis_index("alpha") ^ away) * depth, depth)
        target = out_ref.at[:, pl.ds(row, depth), :] if slot is None else out_ref.at[slot, pl.ds(row, depth), :]
        copies.append(pltpu.make_async_copy(shard, target, sem.at[at]))
    for copy in copies:
        copy.start()
    for copy in copies:
        copy.wait()
    for slot in range(slots):
        for u in range(tile // BLOCK):
            for v in range(tile // BLOCK):
                rows, cols = pl.ds(u * BLOCK, BLOCK), pl.ds(v * BLOCK, BLOCK)
                out_ref[slot, rows, cols] = masked(out_ref[slot, rows, cols], mask_ref[slot, u, v])


def placed_weights(mask, pieces, tile):
    where = tuple(key for key, _ in pieces)
    arrays = [array for _, array in pieces]
    out = jax.ShapeDtypeStruct((mask.shape[0], tile, tile), jnp.bfloat16)
    return pl.pallas_call(
        functools.partial(place_kernel, where),
        in_specs=[SMEM] + [ANY] * len(arrays),
        out_specs=VMEM,
        out_shape=out,
        scratch_shapes=[pltpu.SemaphoreType.DMA((len(arrays),))],
        compiler_params=params(16),
        cost_estimate=cost(0, 4 * out.size),
        name="place",
    )(mask, *arrays)


def alpha_sum(partner_ref, weights_ref, tiles, out_ref):
    for at, source in enumerate(level_sources("alpha", range(len(tiles) // 2))):
        slot = slot_of(partner_ref, source)

        @pl.when(slot >= 0)
        def _():
            left = weights_ref[jnp.maximum(slot, 0)]
            out_ref[...] += (dot(left, tiles[2 * at][...]) + dot(left, tiles[2 * at + 1][...])) * (1.0 / SCALE)


def alpha_first_kernel(count, partner_ref, weights_ref, *refs):
    tiles, (total_ref, out_ref) = refs[: 2 * count], refs[2 * count :]
    out_ref[...] = total_ref[...]
    alpha_sum(partner_ref, weights_ref, tiles, out_ref)


def alpha_second_kernel(count, partner_ref, weights_ref, *refs):
    tiles, (total_ref, ratio_ref, out_ref, final_ref) = refs[: 2 * count], refs[2 * count :]
    out_ref[...] = total_ref[...]
    alpha_sum(partner_ref, weights_ref, tiles, out_ref)

    @pl.when(pl.program_id(0) == 0)
    def _():
        final_ref[...] = out_ref[...] * ratio_ref[...]


def alpha_specs(weights, tiles, rows):
    slots, tile, depth = weights.shape
    whole = pl.BlockSpec((depth, tile), lambda i: (0, 0))
    return [pl.BlockSpec((slots, rows, depth), lambda i: (0, i, 0))] + [whole] * (2 * len(tiles))


def alpha_first(partner, weights, tiles, total, rows):
    count = len(tiles)
    block = pl.BlockSpec((rows, total.shape[1]), lambda i: (i, 0))
    return pl.pallas_call(
        functools.partial(alpha_first_kernel, count),
        grid=(total.shape[0] // rows,),
        in_specs=[SMEM] + alpha_specs(weights, tiles, rows) + [block],
        out_specs=block,
        out_shape=jax.ShapeDtypeStruct(total.shape, jnp.float32),
        input_output_aliases={2 + 2 * count: 0},
        compiler_params=params(24),
        cost_estimate=cost(4 * count * weights.shape[2] * total.size, 8 * total.size),
        name="alpha_first",
    )(partner, weights, *[part for pair in tiles for part in pair], total)


def alpha_second(partner, weights, tiles, total, ratio, rows):
    count = len(tiles)
    block = pl.BlockSpec((rows, total.shape[1]), lambda i: (i, 0))
    top = pl.BlockSpec((rows, total.shape[1]), lambda i: (0, 0))
    shape = jax.ShapeDtypeStruct(total.shape, jnp.float32)
    return pl.pallas_call(
        functools.partial(alpha_second_kernel, count),
        grid=(total.shape[0] // rows,),
        in_specs=[SMEM] + alpha_specs(weights, tiles, rows) + [block, top],
        out_specs=[block, top],
        out_shape=[shape, shape],
        input_output_aliases={2 + 2 * count: 0},
        compiler_params=params(24),
        cost_estimate=cost(4 * count * weights.shape[2] * total.size, 8 * total.size),
        name="alpha_second",
    )(partner, weights, *[part for pair in tiles for part in pair], total, ratio)


def beta_kernel(plain, levels, turned, final, partner_ref, weights_ref, *refs):
    sources, refs = refs[: plain + 2 * levels + 2], refs[plain + 2 * levels + 2 :]
    total_ref, out_ref = refs[0], refs[-1]
    out_ref[...] = total_ref[...]
    origins = level_sources("beta", range(plain + levels)) + [cycle_source("beta", turned)]
    for at, origin in enumerate(origins):
        slot = slot_of(partner_ref, origin)

        @pl.when(slot >= 0)
        def _():
            right = weights_ref[jnp.maximum(slot, 0)]
            if at < plain:
                high, low = halves(sources[at][...])
                out_ref[...] += dot(high, right) + dot(low, right)
            else:
                first = plain + 2 * (at - plain)
                out_ref[...] += (dot(sources[first][...], right) + dot(sources[first + 1][...], right)) * (1.0 / SCALE)

    if final:
        out_ref[...] = out_ref[...] * refs[1][...]


def beta_products(partner, weights, plain, pairs, chunk, turned, total, start, rows, ratio=None, out=None):
    width = total.shape[1]
    depth = chunk[0].shape[0]
    offset = start // rows
    here = pl.BlockSpec((rows, width), lambda i: (i + offset, 0))
    local_block = pl.BlockSpec((rows, width), lambda i: (i, 0))
    count = len(plain) + len(pairs) + 1
    sources = list(plain) + [part for pair in pairs for part in pair] + list(chunk)
    final = ratio is not None
    operands = [partner, weights, *sources, total] + ([ratio, out] if final else [])
    return pl.pallas_call(
        functools.partial(beta_kernel, len(plain), len(pairs), turned, final),
        grid=(depth // rows,),
        in_specs=[SMEM, VMEM]
        + [here] * (len(sources) - 2)
        + [local_block] * 2
        + [here]
        + ([here, ANY] if final else []),
        out_specs=here,
        out_shape=jax.ShapeDtypeStruct(total.shape, jnp.float32),
        input_output_aliases={len(operands) - 1: 0},
        compiler_params=params(24),
        cost_estimate=cost(4 * count * depth * width * width, 4 * depth * width * (count + 2)),
        name="beta_products",
    )(*operands)


def gather_pieces(shard):
    size = lax.axis_size("alpha")
    pieces = [((0, None), shard)]
    whole = {}
    bit = 1
    while bit < size:
        whole[bit] = flip(shard, "alpha", bit)
        pieces.append(((bit, None), whole[bit]))
        bit *= 2
    single = {(away, slot): held[slot] for away, held in whole.items() for slot in range(2)}
    for away in sorted(range(1, size), key=lambda k: bin(k).count("1")):
        if away in whole:
            continue
        for slot in range(2):
            hop = away & -away if slot == 0 else 1 << (away.bit_length() - 1)
            single[(away, slot)] = flip(single[(away ^ hop, slot)], "alpha", hop)
            pieces.append(((away, slot), single[(away, slot)]))
    return pieces


def local(
    ci_vector,
    diagonal,
    energy,
    alpha_partner,
    alpha_coupling,
    alpha_mask,
    beta_partner,
    beta_coupling,
    beta_mask,
):
    tile, _ = ci_vector.shape
    beta_size = lax.axis_size("beta")
    beta_bits = beta_size.bit_length() - 1
    alpha_bits = lax.axis_size("alpha").bit_length() - 1
    half, quarter = tile // 2, tile // 4
    cut = (tile // BLOCK + 1) // 2 * BLOCK

    early = [(0, quarter), (quarter, tile - quarter)]
    late = [(0, half), (half, quarter), (half + quarter, quarter)]
    depths = [(0, cut), (cut, tile - cut)]
    first, second = cycle_pairs(beta_size, False), cycle_pairs(beta_size, True)

    rest = ci_vector
    from_first = []
    for a, n in early:
        piece = short(rest[a : a + n])
        rest, piece = lax.optimization_barrier((rest, piece))
        from_first.append(lax.ppermute(piece, "beta", first))
    pieces = gather_pieces(beta_coupling[0])
    from_core = flip(ci_vector, "beta", 1)
    from_alpha = []
    for a, n in depths:
        piece = short(rest[a : a + n])
        arrived = []
        for level in range(alpha_bits):
            arrived.append(flip(piece, "alpha", 1 << level))
        from_alpha.append(arrived)
    from_second = []
    for a, n in late:
        piece = short(rest[a : a + n])
        from_second.append(lax.ppermute(piece, "beta", second))
    from_levels = []
    for level in range(1, beta_bits - 2):
        from_levels.append(flip(short(rest), "beta", 1 << level))

    alpha_weights = turned_weights(alpha_mask[0], alpha_coupling[0], cut)
    beta_weights = placed_weights(beta_mask[0], pieces, tile)
    gap = diagonal - energy[0]
    ratio = gap / (gap * gap + 0.0625)
    total = -energy[0] * ci_vector
    levels = [split(value) for value in from_levels]
    for (start, _), arrived in zip(early, from_first):
        total = beta_products(
            beta_partner, beta_weights, [from_core], levels, split(arrived), False, total, start, quarter
        )
    tiles = [split(value) for value in from_alpha[0]]
    total = alpha_first(alpha_partner, alpha_weights[0], tiles, total, half)
    total = beta_products(beta_partner, beta_weights, [], [], split(from_second[0]), True, total, 0, half)
    tiles = [split(value) for value in from_alpha[1]]
    total, out = alpha_second(alpha_partner, alpha_weights[1], tiles, total, ratio, half)
    for at in (1, 2):
        out = beta_products(
            beta_partner, beta_weights, [], [], split(from_second[at]), True,
            total, late[at][0], quarter, ratio, out,
        )
    return out


def solution(mesh):
    return jax.shard_map(
        local,
        mesh=mesh,
        in_specs=(
            P("alpha", "beta"),
            P("alpha", "beta"),
            P(),
            P("alpha", None),
            P("alpha", None, None, None),
            P("alpha", None, None, None),
            P("beta", None),
            P("beta", None, "alpha", None),
            P("beta", None, None, None),
        ),
        out_specs=P("alpha", "beta"),
        check_vma=False,
    )
```

```python
import functools

import jax
import jax.numpy as jnp
from jax import lax
from jax.experimental import pallas as pl
from jax.experimental.pallas import tpu as pltpu
from jax.sharding import PartitionSpec as P


BLOCK = 128
SCALE = 8192.0
VMEM = pl.BlockSpec(memory_space=pltpu.VMEM)
SMEM = pl.BlockSpec(memory_space=pltpu.SMEM)
ANY = pl.BlockSpec(memory_space=pl.ANY)


def params(mib):
    return pltpu.CompilerParams(vmem_limit_bytes=mib * 2**20)


def cost(flops, moved):
    return pl.CostEstimate(flops=flops, bytes_accessed=moved, transcendentals=0)


def flip(value, axis, bit):
    return lax.ppermute(value, axis, [(i, i ^ bit) for i in range(lax.axis_size(axis))])


def short(value):
    return (value * SCALE).astype(jnp.float16)


def split(value):
    value = value.astype(jnp.float32)
    high = lax.reduce_precision(value, 8, 7)
    return high.astype(jnp.bfloat16), (value - high).astype(jnp.bfloat16)


def halves(value):
    high = value.astype(jnp.bfloat16)
    return high, (value - high.astype(jnp.float32)).astype(jnp.bfloat16)


def dot(left, right):
    return jnp.dot(left, right, preferred_element_type=jnp.float32)


def cycle_pairs(size, turned):
    low, high = size >> 2, size >> 1
    return [
        (i, i ^ (high if (bool(i & low) ^ bool(i & high)) ^ turned else low))
        for i in range(size)
    ]


def level_source(axis, level):
    return lax.axis_index(axis) ^ (1 << level)


def cycle_source(axis, turned):
    size = lax.axis_size(axis)
    index = lax.axis_index(axis)
    low, high = size >> 2, size >> 1
    odd = ((index // low) + (index // high)) % 2 == 1
    return index ^ (jnp.where(odd, high, low) if turned else jnp.where(odd, low, high))


def slot_of(partner_ref, source):
    return jnp.where(partner_ref[0, 0] == source, 0, jnp.where(partner_ref[0, 1] == source, 1, -1))


def masked(block, bit):
    return (block.astype(jnp.float32) * bit.astype(jnp.float32)).astype(jnp.bfloat16)


def turn_kernel(cut, mask_ref, coupling_ref, *out_refs):
    slot = pl.program_id(0)
    blocks = coupling_ref.shape[1] // BLOCK
    for u in range(blocks):
        for v in range(blocks):
            rows, cols = pl.ds(u * BLOCK, BLOCK), pl.ds(v * BLOCK, BLOCK)
            out_ref, to = (out_refs[0], u) if u < cut else (out_refs[1], u - cut)
            out_ref[0, cols, pl.ds(to * BLOCK, BLOCK)] = masked(coupling_ref[0, rows, cols], mask_ref[slot, u, v]).T


def turned_weights(mask, coupling, cut):
    slots, tile, _ = coupling.shape
    depths = (cut, tile - cut)
    return pl.pallas_call(
        functools.partial(turn_kernel, cut // BLOCK),
        grid=(slots,),
        in_specs=[SMEM, pl.BlockSpec((1, tile, tile), lambda s: (s, 0, 0))],
        out_specs=[pl.BlockSpec((1, tile, depth), lambda s: (s, 0, 0)) for depth in depths],
        out_shape=[jax.ShapeDtypeStruct((slots, tile, depth), coupling.dtype) for depth in depths],
        compiler_params=params(16),
        cost_estimate=cost(0, 4 * coupling.size),
        name="turn",
    )(mask, coupling)


def place_kernel(where, fresh, mask_ref, *refs):
    shards, out_ref, sem = refs[: len(where)], refs[-2], refs[-1]
    copies, rows = [], []
    for at, ((away, slot), shard) in enumerate(zip(where, shards)):
        depth = shard.shape[-2]
        row = pl.multiple_of((lax.axis_index("alpha") ^ away) * depth, depth)
        rows.append((row, depth, slot))
        target = out_ref.at[:, pl.ds(row, depth), :] if slot is None else out_ref.at[slot, pl.ds(row, depth), :]
        copies.append(pltpu.make_async_copy(shard, target, sem.at[at]))
    for copy in copies:
        copy.start()
    for copy in copies:
        copy.wait()
    if fresh:
        return
    slots, tile, _ = out_ref.shape
    for slot in range(slots):
        for u in range(tile // BLOCK):
            for v in range(tile // BLOCK):
                rows, cols = pl.ds(u * BLOCK, BLOCK), pl.ds(v * BLOCK, BLOCK)
                out_ref[slot, rows, cols] = masked(out_ref[slot, rows, cols], mask_ref[slot, u, v])


def placed_weights(mask, pieces, tile, held=None):
    where = tuple(key for key, _ in pieces)
    arrays = [array for _, array in pieces]
    out = jax.ShapeDtypeStruct((mask.shape[0], tile, tile), jnp.bfloat16)
    fresh = held is None
    return pl.pallas_call(
        functools.partial(place_kernel, where, fresh),
        in_specs=[SMEM] + [ANY] * len(arrays) + ([] if fresh else [VMEM]),
        out_specs=VMEM,
        out_shape=out,
        scratch_shapes=[pltpu.SemaphoreType.DMA((len(arrays),))],
        input_output_aliases={} if fresh else {1 + len(arrays): 0},
        compiler_params=params(12),
        cost_estimate=cost(0, 2 * out.size),
        name="place",
    )(mask, *arrays, *([] if fresh else [held]))


def alpha_sum(partner_ref, weights_ref, tiles, out_ref):
    for at in range(len(tiles) // 2):
        slot = slot_of(partner_ref, level_source("alpha", at))

        @pl.when(slot >= 0)
        def _():
            left = weights_ref[jnp.maximum(slot, 0)]
            out_ref[...] += (dot(left, tiles[2 * at][...]) + dot(left, tiles[2 * at + 1][...])) * (1.0 / SCALE)


def alpha_first_kernel(count, partner_ref, weights_ref, *refs):
    tiles, (total_ref, out_ref) = refs[: 2 * count], refs[2 * count :]
    out_ref[...] = total_ref[...]
    alpha_sum(partner_ref, weights_ref, tiles, out_ref)


def alpha_second_kernel(count, partner_ref, weights_ref, *refs):
    tiles, (total_ref, ratio_ref, out_ref, final_ref) = refs[: 2 * count], refs[2 * count :]
    out_ref[...] = total_ref[...]
    alpha_sum(partner_ref, weights_ref, tiles, out_ref)

    @pl.when(pl.program_id(0) == 0)
    def _():
        final_ref[...] = out_ref[...] * ratio_ref[...]


def alpha_specs(weights, tiles, rows):
    slots, tile, depth = weights.shape
    whole = pl.BlockSpec((depth, tile), lambda i: (0, 0))
    return [pl.BlockSpec((slots, rows, depth), lambda i: (0, i, 0))] + [whole] * (2 * len(tiles))


def alpha_first(partner, weights, tiles, total, rows):
    count = len(tiles)
    block = pl.BlockSpec((rows, total.shape[1]), lambda i: (i, 0))
    return pl.pallas_call(
        functools.partial(alpha_first_kernel, count),
        grid=(total.shape[0] // rows,),
        in_specs=[SMEM] + alpha_specs(weights, tiles, rows) + [block],
        out_specs=block,
        out_shape=jax.ShapeDtypeStruct(total.shape, jnp.float32),
        input_output_aliases={2 + 2 * count: 0},
        compiler_params=params(24),
        cost_estimate=cost(4 * count * weights.shape[2] * total.size, 8 * total.size),
        name="alpha_first",
    )(partner, weights, *[part for pair in tiles for part in pair], total)


def alpha_second(partner, weights, tiles, total, ratio, rows):
    count = len(tiles)
    block = pl.BlockSpec((rows, total.shape[1]), lambda i: (i, 0))
    top = pl.BlockSpec((rows, total.shape[1]), lambda i: (0, 0))
    shape = jax.ShapeDtypeStruct(total.shape, jnp.float32)
    return pl.pallas_call(
        functools.partial(alpha_second_kernel, count),
        grid=(total.shape[0] // rows,),
        in_specs=[SMEM] + alpha_specs(weights, tiles, rows) + [block, top],
        out_specs=[block, top],
        out_shape=[shape, shape],
        input_output_aliases={2 + 2 * count: 0},
        compiler_params=params(24),
        cost_estimate=cost(4 * count * weights.shape[2] * total.size, 8 * total.size),
        name="alpha_second",
    )(partner, weights, *[part for pair in tiles for part in pair], total, ratio)


def beta_kernel(origins, plain, final, partner_ref, weights_ref, *refs):
    sources, refs = refs[: plain + 2 * (len(origins) - plain)], refs[plain + 2 * (len(origins) - plain) :]
    total_ref, out_ref = refs[0], refs[-1]
    out_ref[...] = total_ref[...]
    for at, origin in enumerate(origins):
        slot = slot_of(partner_ref, origin())

        @pl.when(slot >= 0)
        def _():
            right = weights_ref[jnp.maximum(slot, 0)]
            if at < plain:
                high, low = halves(sources[at][...])
                out_ref[...] += dot(high, right) + dot(low, right)
            else:
                first = plain + 2 * (at - plain)
                out_ref[...] += (dot(sources[first][...], right) + dot(sources[first + 1][...], right)) * (1.0 / SCALE)

    if final:
        out_ref[...] = out_ref[...] * refs[1][...]


def beta_products(partner, weights, origins, plain, pairs, total, start, rows, ratio=None, out=None):
    width = total.shape[1]
    sources = list(plain) + [part for pair in pairs for part in pair]
    depth = sources[0].shape[0]
    offset = start // rows
    here = pl.BlockSpec((rows, width), lambda i: (i + offset, 0))
    local_block = pl.BlockSpec((rows, width), lambda i: (i, 0))
    final = ratio is not None
    operands = [partner, weights, *sources, total] + ([ratio, out] if final else [])
    return pl.pallas_call(
        functools.partial(beta_kernel, origins, len(plain), final),
        grid=(depth // rows,),
        in_specs=[SMEM, VMEM] + [local_block] * len(sources) + [here] + ([here, ANY] if final else []),
        out_specs=here,
        out_shape=jax.ShapeDtypeStruct(total.shape, jnp.float32),
        input_output_aliases={len(operands) - 1: 0},
        compiler_params=params(24),
        cost_estimate=cost(4 * len(origins) * depth * width * width, 4 * depth * width * (len(origins) + 2)),
        name="beta_products",
    )(*operands)


def gather_pieces(shard):
    size = lax.axis_size("alpha")
    pieces = [((0, None), shard)]
    whole = {}
    bit = 1
    while bit < size:
        whole[bit] = flip(shard, "alpha", bit)
        pieces.append(((bit, None), whole[bit]))
        bit *= 2
    single = {(away, slot): held[slot] for away, held in whole.items() for slot in range(2)}
    for away in sorted(range(1, size), key=lambda k: bin(k).count("1")):
        if away in whole:
            continue
        for slot in range(2):
            hop = away & -away if slot == 0 else 1 << (away.bit_length() - 1)
            single[(away, slot)] = flip(single[(away ^ hop, slot)], "alpha", hop)
            pieces.append(((away, slot), single[(away, slot)]))
    return pieces


def local(
    ci_vector,
    diagonal,
    energy,
    alpha_partner,
    alpha_coupling,
    alpha_mask,
    beta_partner,
    beta_coupling,
    beta_mask,
):
    tile, _ = ci_vector.shape
    beta_size = lax.axis_size("beta")
    beta_bits = beta_size.bit_length() - 1
    alpha_bits = lax.axis_size("alpha").bit_length() - 1
    half, quarter = tile // 2, tile // 4
    cut = (tile // BLOCK + 1) // 2 * BLOCK

    early = [(0, quarter), (quarter, tile - quarter)]
    late = [(0, half), (half, quarter), (half + quarter, quarter)]
    depths = [(0, cut), (cut, tile - cut)]
    first, second = cycle_pairs(beta_size, False), cycle_pairs(beta_size, True)

    rest = ci_vector
    from_first = []
    for a, n in early:
        piece = short(rest[a : a + n])
        rest, piece = lax.optimization_barrier((rest, piece))
        from_first.append(lax.ppermute(piece, "beta", first))
    pieces = gather_pieces(beta_coupling[0])
    from_core = flip(ci_vector, "beta", 1)
    from_alpha = []
    for a, n in depths:
        piece = short(rest[a : a + n])
        arrived = []
        for level in range(alpha_bits):
            arrived.append(flip(piece, "alpha", 1 << level))
        from_alpha.append(arrived)
    from_second = []
    for a, n in late:
        piece = short(rest[a : a + n])
        from_second.append(lax.ppermute(piece, "beta", second))
    from_levels = []
    for level in range(1, beta_bits - 2):
        from_levels.append(flip(short(rest), "beta", 1 << level))

    alpha_weights = turned_weights(alpha_mask[0], alpha_coupling[0], cut)
    direct = [piece for piece in pieces if piece[0][1] is None]
    routed = [piece for piece in pieces if piece[0][1] is not None]
    beta_weights = placed_weights(beta_mask[0], direct, tile)
    beta_weights = placed_weights(beta_mask[0], routed, tile, beta_weights)
    gap = diagonal - energy[0]
    ratio = gap / (gap * gap + 0.0625)
    total = -energy[0] * ci_vector
    gap = diagonal - energy[0]
    ratio = gap / (gap * gap + 0.0625)
    total = -energy[0] * ci_vector
    origins = [functools.partial(level_source, "beta", level) for level in range(beta_bits - 2)]
    from_cycle = [functools.partial(cycle_source, "beta", turned) for turned in (False, True)]
    levels = [split(value) for value in from_levels]
    total = beta_products(beta_partner, beta_weights, origins, [from_core], levels, total, 0, half)
    for (start, _), arrived in zip(early, from_first):
        total = beta_products(beta_partner, beta_weights, from_cycle[:1], [], [split(arrived)], total, start, quarter)
    tiles = [split(value) for value in from_alpha[0]]
    total = alpha_first(alpha_partner, alpha_weights[0], tiles, total, half)
    total = beta_products(
        beta_partner, beta_weights, from_cycle[1:], [], [split(from_second[0])], total, 0, half
    )
    tiles = [split(value) for value in from_alpha[1]]
    total, out = alpha_second(alpha_partner, alpha_weights[1], tiles, total, ratio, half)
    for at in (1, 2):
        start, depth = late[at]
        out = beta_products(
            beta_partner, beta_weights, from_cycle[1:], [], [split(from_second[at])],
            total, start, depth, ratio, out,
        )
    return out


def solution(mesh):
    return jax.shard_map(
        local,
        mesh=mesh,
        in_specs=(
            P("alpha", "beta"),
            P("alpha", "beta"),
            P(),
            P("alpha", None),
            P("alpha", None, None, None),
            P("alpha", None, None, None),
            P("beta", None),
            P("beta", None, "alpha", None),
            P("beta", None, None, None),
        ),
        out_specs=P("alpha", "beta"),
        check_vma=False,
    )
```

```python
import functools

import jax
import jax.numpy as jnp
from jax import lax
from jax.experimental import pallas as pl
from jax.experimental.pallas import tpu as pltpu
from jax.sharding import PartitionSpec as P


BLOCK = 128
SCALE = 8192.0
VMEM = pl.BlockSpec(memory_space=pltpu.VMEM)
SMEM = pl.BlockSpec(memory_space=pltpu.SMEM)
ANY = pl.BlockSpec(memory_space=pl.ANY)


def params(mib):
    return pltpu.CompilerParams(vmem_limit_bytes=mib * 2**20)


def cost(flops, moved):
    return pl.CostEstimate(flops=flops, bytes_accessed=moved, transcendentals=0)


def flip(value, axis, bit):
    return lax.ppermute(value, axis, [(i, i ^ bit) for i in range(lax.axis_size(axis))])


def short(value):
    return (value * SCALE).astype(jnp.float16)


def split(value):
    value = value.astype(jnp.float32)
    high = lax.reduce_precision(value, 8, 7)
    return high.astype(jnp.bfloat16), (value - high).astype(jnp.bfloat16)


def halves(value):
    high = value.astype(jnp.bfloat16)
    return high, (value - high.astype(jnp.float32)).astype(jnp.bfloat16)


def dot(left, right):
    return jnp.dot(left, right, preferred_element_type=jnp.float32)


def cycle_pairs(size, turned):
    low, high = size >> 2, size >> 1
    return [
        (i, i ^ (high if (bool(i & low) ^ bool(i & high)) ^ turned else low))
        for i in range(size)
    ]


def level_source(axis, level):
    return lax.axis_index(axis) ^ (1 << level)


def cycle_source(axis, turned):
    size = lax.axis_size(axis)
    index = lax.axis_index(axis)
    low, high = size >> 2, size >> 1
    odd = ((index // low) + (index // high)) % 2 == 1
    return index ^ (jnp.where(odd, high, low) if turned else jnp.where(odd, low, high))


def slot_of(partner_ref, source):
    return jnp.where(partner_ref[0, 0] == source, 0, jnp.where(partner_ref[0, 1] == source, 1, -1))


def masked(block, bit):
    return (block.astype(jnp.float32) * bit.astype(jnp.float32)).astype(jnp.bfloat16)


def turn_kernel(cut, mask_ref, coupling_ref, *out_refs):
    slot = pl.program_id(0)
    blocks = coupling_ref.shape[1] // BLOCK
    for u in range(blocks):
        for v in range(blocks):
            rows, cols = pl.ds(u * BLOCK, BLOCK), pl.ds(v * BLOCK, BLOCK)
            out_ref, to = (out_refs[0], u) if u < cut else (out_refs[1], u - cut)
            out_ref[0, cols, pl.ds(to * BLOCK, BLOCK)] = masked(coupling_ref[0, rows, cols], mask_ref[slot, u, v]).T


def turned_weights(mask, coupling, cut):
    slots, tile, _ = coupling.shape
    depths = (cut, tile - cut)
    return pl.pallas_call(
        functools.partial(turn_kernel, cut // BLOCK),
        grid=(slots,),
        in_specs=[SMEM, pl.BlockSpec((1, tile, tile), lambda s: (s, 0, 0))],
        out_specs=[pl.BlockSpec((1, tile, depth), lambda s: (s, 0, 0)) for depth in depths],
        out_shape=[jax.ShapeDtypeStruct((slots, tile, depth), coupling.dtype) for depth in depths],
        compiler_params=params(16),
        cost_estimate=cost(0, 4 * coupling.size),
        name="turn",
    )(mask, coupling)


def place_kernel(where, fresh, mask_ref, *refs):
    shards, out_ref, sem = refs[: len(where)], refs[-2], refs[-1]
    copies, rows = [], []
    for at, ((away, slot), shard) in enumerate(zip(where, shards)):
        depth = shard.shape[-2]
        row = pl.multiple_of((lax.axis_index("alpha") ^ away) * depth, depth)
        rows.append((row, depth, slot))
        target = out_ref.at[:, pl.ds(row, depth), :] if slot is None else out_ref.at[slot, pl.ds(row, depth), :]
        copies.append(pltpu.make_async_copy(shard, target, sem.at[at]))
    for copy in copies:
        copy.start()
    for copy in copies:
        copy.wait()
    if fresh:
        return
    slots, tile, _ = out_ref.shape
    for slot in range(slots):
        for u in range(tile // BLOCK):
            for v in range(tile // BLOCK):
                rows, cols = pl.ds(u * BLOCK, BLOCK), pl.ds(v * BLOCK, BLOCK)
                out_ref[slot, rows, cols] = masked(out_ref[slot, rows, cols], mask_ref[slot, u, v])


def placed_weights(mask, pieces, tile, held=None):
    where = tuple(key for key, _ in pieces)
    arrays = [array for _, array in pieces]
    out = jax.ShapeDtypeStruct((mask.shape[0], tile, tile), jnp.bfloat16)
    fresh = held is None
    return pl.pallas_call(
        functools.partial(place_kernel, where, fresh),
        in_specs=[SMEM] + [ANY] * len(arrays) + ([] if fresh else [VMEM]),
        out_specs=VMEM,
        out_shape=out,
        scratch_shapes=[pltpu.SemaphoreType.DMA((len(arrays),))],
        input_output_aliases={} if fresh else {1 + len(arrays): 0},
        compiler_params=params(12),
        cost_estimate=cost(0, 2 * out.size),
        name="place",
    )(mask, *arrays, *([] if fresh else [held]))


def alpha_sum(partner_ref, weights_ref, tiles, out_ref):
    for at in range(len(tiles) // 2):
        slot = slot_of(partner_ref, level_source("alpha", at))

        @pl.when(slot >= 0)
        def _():
            left = weights_ref[jnp.maximum(slot, 0)]
            out_ref[...] += (dot(left, tiles[2 * at][...]) + dot(left, tiles[2 * at + 1][...])) * (1.0 / SCALE)


def alpha_first_kernel(count, partner_ref, weights_ref, *refs):
    tiles, (total_ref, out_ref) = refs[: 2 * count], refs[2 * count :]
    out_ref[...] = total_ref[...]
    alpha_sum(partner_ref, weights_ref, tiles, out_ref)


def alpha_specs(weights, tiles, rows):
    slots, tile, depth = weights.shape
    whole = pl.BlockSpec((depth, tile), lambda i: (0, 0))
    return [pl.BlockSpec((slots, rows, depth), lambda i: (0, i, 0))] + [whole] * (2 * len(tiles))


def alpha_first(partner, weights, tiles, total, rows):
    count = len(tiles)
    block = pl.BlockSpec((rows, total.shape[1]), lambda i: (i, 0))
    return pl.pallas_call(
        functools.partial(alpha_first_kernel, count),
        grid=(total.shape[0] // rows,),
        in_specs=[SMEM] + alpha_specs(weights, tiles, rows) + [block],
        out_specs=block,
        out_shape=jax.ShapeDtypeStruct(total.shape, jnp.float32),
        input_output_aliases={2 + 2 * count: 0},
        compiler_params=params(24),
        cost_estimate=cost(4 * count * weights.shape[2] * total.size, 8 * total.size),
        name="alpha_first",
    )(partner, weights, *[part for pair in tiles for part in pair], total)


def alpha_final_kernel(count, rows, final, partner_ref, weights_ref, *refs):
    tiles, refs = refs[: 2 * count], refs[2 * count :]
    total_ref, out_ref = refs[0], refs[2 if final else 1]
    copies = []
    for start in range(0, out_ref.shape[0], rows):
        here = pl.ds(start, rows)
        out_ref[here, :] = total_ref[here, :]
        for at in range(count):
            slot = slot_of(partner_ref, level_source("alpha", at))

            @pl.when(slot >= 0)
            def _():
                left = weights_ref[jnp.maximum(slot, 0), here, :]
                product = dot(left, tiles[2 * at][...]) + dot(left, tiles[2 * at + 1][...])
                out_ref[here, :] += product * (1.0 / SCALE)

        if final and start == 0:
            held, sem = refs[4], refs[5]
            held[...] = out_ref[here, :] * refs[1][here, :]
            copies.append(pltpu.make_async_copy(held, refs[3].at[here, :], sem))
            copies[-1].start()
    for copy in copies:
        copy.wait()


def alpha_final(partner, weights, tiles, total, rows, ratio=None):
    count = len(tiles)
    final = ratio is not None
    shape = jax.ShapeDtypeStruct(total.shape, jnp.float32)
    scratch = [pltpu.VMEM((rows, total.shape[1]), jnp.float32), pltpu.SemaphoreType.DMA] if final else []
    return pl.pallas_call(
        functools.partial(alpha_final_kernel, count, rows, final),
        in_specs=[SMEM] + [VMEM] * (2 * count + 2 + final),
        out_specs=[VMEM, ANY] if final else VMEM,
        out_shape=[shape, shape] if final else shape,
        scratch_shapes=scratch,
        input_output_aliases={2 + 2 * count: 0},
        compiler_params=params(20),
        cost_estimate=cost(4 * count * weights.shape[2] * total.size, 8 * total.size),
        name="alpha_products",
    )(partner, weights, *[part for pair in tiles for part in pair], total, *([ratio] if final else []))


def beta_kernel(origins, plain, final, partner_ref, weights_ref, *refs):
    sources, refs = refs[: plain + 2 * (len(origins) - plain)], refs[plain + 2 * (len(origins) - plain) :]
    total_ref, out_ref = refs[0], refs[-1]
    out_ref[...] = total_ref[...]
    for at, origin in enumerate(origins):
        slot = slot_of(partner_ref, origin())

        @pl.when(slot >= 0)
        def _():
            right = weights_ref[jnp.maximum(slot, 0)]
            if at < plain:
                high, low = halves(sources[at][...])
                out_ref[...] += dot(high, right) + dot(low, right)
            else:
                first = plain + 2 * (at - plain)
                out_ref[...] += (dot(sources[first][...], right) + dot(sources[first + 1][...], right)) * (1.0 / SCALE)

    if final:
        out_ref[...] = out_ref[...] * refs[1][...]


def beta_products(partner, weights, origins, plain, pairs, total, start, rows, ratio=None, out=None):
    width = total.shape[1]
    sources = list(plain) + [part for pair in pairs for part in pair]
    depth = sources[0].shape[0]
    offset = start // rows
    here = pl.BlockSpec((rows, width), lambda i: (i + offset, 0))
    local_block = pl.BlockSpec((rows, width), lambda i: (i, 0))
    final = ratio is not None
    operands = [partner, weights, *sources, total] + ([ratio, out] if final else [])
    return pl.pallas_call(
        functools.partial(beta_kernel, origins, len(plain), final),
        grid=(depth // rows,),
        in_specs=[SMEM, VMEM] + [local_block] * len(sources) + [here] + ([here, ANY] if final else []),
        out_specs=here,
        out_shape=jax.ShapeDtypeStruct(total.shape, jnp.float32),
        input_output_aliases={len(operands) - 1: 0},
        compiler_params=params(24),
        cost_estimate=cost(4 * len(origins) * depth * width * width, 4 * depth * width * (len(origins) + 2)),
        name="beta_products",
    )(*operands)


def gather_pieces(shard):
    size = lax.axis_size("alpha")
    pieces = [((0, None), shard)]
    whole = {}
    bit = 1
    while bit < size:
        whole[bit] = flip(shard, "alpha", bit)
        pieces.append(((bit, None), whole[bit]))
        bit *= 2
    single = {(away, slot): held[slot] for away, held in whole.items() for slot in range(2)}
    for away in sorted(range(1, size), key=lambda k: bin(k).count("1")):
        if away in whole:
            continue
        for slot in range(2):
            hop = away & -away if slot == 0 else 1 << (away.bit_length() - 1)
            single[(away, slot)] = flip(single[(away ^ hop, slot)], "alpha", hop)
            pieces.append(((away, slot), single[(away, slot)]))
    return pieces


def local(
    ci_vector,
    diagonal,
    energy,
    alpha_partner,
    alpha_coupling,
    alpha_mask,
    beta_partner,
    beta_coupling,
    beta_mask,
):
    tile, _ = ci_vector.shape
    beta_size = lax.axis_size("beta")
    beta_bits = beta_size.bit_length() - 1
    alpha_bits = lax.axis_size("alpha").bit_length() - 1
    half, quarter = tile // 2, tile // 4
    cut = (tile // BLOCK + 1) // 2 * BLOCK

    early = [(0, quarter), (quarter, tile - quarter)]
    late = [(0, half), (half, quarter), (half + quarter, quarter)]
    depths = [(0, cut), (cut, tile - cut)]
    first, second = cycle_pairs(beta_size, False), cycle_pairs(beta_size, True)

    rest = ci_vector
    from_first = []
    for a, n in early:
        piece = short(rest[a : a + n])
        rest, piece = lax.optimization_barrier((rest, piece))
        from_first.append(lax.ppermute(piece, "beta", first))
    pieces = gather_pieces(beta_coupling[0])
    from_core = flip(ci_vector, "beta", 1)
    from_alpha = []
    for a, n in depths:
        piece = short(rest[a : a + n])
        arrived = []
        for level in range(alpha_bits):
            arrived.append(flip(piece, "alpha", 1 << level))
        from_alpha.append(arrived)
    from_second = []
    for a, n in late:
        piece = short(rest[a : a + n])
        from_second.append(lax.ppermute(piece, "beta", second))
    from_levels = []
    for level in range(1, beta_bits - 2):
        from_levels.append(flip(short(rest), "beta", 1 << level))

    alpha_weights = turned_weights(alpha_mask[0], alpha_coupling[0], cut)
    direct = [piece for piece in pieces if piece[0][1] is None]
    routed = [piece for piece in pieces if piece[0][1] is not None]
    beta_weights = placed_weights(beta_mask[0], direct, tile)
    beta_weights = placed_weights(beta_mask[0], routed, tile, beta_weights)
    gap = diagonal - energy[0]
    ratio = gap / (gap * gap + 0.0625)
    total = -energy[0] * ci_vector
    gap = diagonal - energy[0]
    ratio = gap / (gap * gap + 0.0625)
    total = -energy[0] * ci_vector
    origins = [functools.partial(level_source, "beta", level) for level in range(beta_bits - 2)]
    from_cycle = [functools.partial(cycle_source, "beta", turned) for turned in (False, True)]
    levels = [split(value) for value in from_levels]
    total = beta_products(beta_partner, beta_weights, origins, [from_core], levels, total, 0, half)
    for (start, _), arrived in zip(early, from_first):
        total = beta_products(beta_partner, beta_weights, from_cycle[:1], [], [split(arrived)], total, start, quarter)
    tiles = [split(value) for value in from_alpha[0]]
    total = alpha_first(alpha_partner, alpha_weights[0], tiles, total, half)
    total = beta_products(
        beta_partner, beta_weights, from_cycle[1:], [], [split(from_second[0])], total, 0, half
    )
    tiles = [split(value) for value in from_alpha[1]]
    total, out = alpha_final(alpha_partner, alpha_weights[1], tiles, total, half, ratio)
    for at in (1, 2):
        start, depth = late[at]
        out = beta_products(
            beta_partner, beta_weights, from_cycle[1:], [], [split(from_second[at])],
            total, start, depth, ratio, out,
        )
    return out


def solution(mesh):
    return jax.shard_map(
        local,
        mesh=mesh,
        in_specs=(
            P("alpha", "beta"),
            P("alpha", "beta"),
            P(),
            P("alpha", None),
            P("alpha", None, None, None),
            P("alpha", None, None, None),
            P("beta", None),
            P("beta", None, "alpha", None),
            P("beta", None, None, None),
        ),
        out_specs=P("alpha", "beta"),
        check_vma=False,
    )
```
